32 devices in a mesh: dp: 4 (over z), row: 2 (over x), col: 4 (over y, core).
Axes of the slice: x: 2, y: 2, z: 4, core: 2. Of those that a mesh axis runs over, the one named last changes fastest.
Arguments:
- activations: bfloat16 [8192, 1024], P(('dp', 'row', 'col')), may hold values from -6 to 6
- upstream_grad: bfloat16 [8192, 1024], P(('dp', 'row', 'col')), may hold values from -6 to 6
- w_qkv: bfloat16 [1024, 3, 1024], P(('dp', 'row'), None, 'col'), may hold values from -0.1875 to 0.1875
- w_out_attn: bfloat16 [1024, 1024], P('col', ('dp', 'row')), may hold values from -3 to 3
- w_in: bfloat16 [1024, 2, 2624], P(('dp', 'row'), None, 'col'), may hold values from -0.1875 to 0.1875
- w_out_mlp: bfloat16 [2624, 1024], P('col', ('dp', 'row')), may hold values from -0.125 to 0.125
- gain_attn: float32 [1024], replicated, may hold values from 0.5 to 1.5
- gain_mlp: float32 [1024], replicated, may hold values from 0.5 to 1.5
- lengths: int32 [8], replicated, may hold values from 1 to 1024, 5120 in all
- seq_order: int32 [8], replicated, may hold values from 0 to 7, each once
Outputs:
- block_out: bfloat16 [8192, 1024], P(('dp', 'row', 'col'))
- grad_input: bfloat16 [8192, 1024], P(('dp', 'row', 'col'))
- grad_w_qkv: float32 [1024, 3, 1024], P(('dp', 'row'), None, 'col')
- grad_w_out_attn: float32 [1024, 1024], P('col', ('dp', 'row'))
- grad_w_in: float32 [1024, 2, 2624], P(('dp', 'row'), None, 'col')
- grad_w_out_mlp: float32 [2624, 1024], P('col', ('dp', 'row'))
- grad_gain_attn: float32 [1024], replicated
- grad_gain_mlp: float32 [1024], replicated
The draws below stay inside these ranges and needn't reach their ends.
Inputs may be any that keep to these rules, and one draw needn't show every extreme that they name: `lengths`: a sequence's length; the longest is exactly 1024. `seq_order`: each sequence number once.
All inputs are finite; a program needn't handle non-finite values.
Results may differ from the reference program's by a relative error of at most 0.015.
Values may be sent and summed in bfloat16 or wider, within the bound.
No kernel may reach another device: no remote copies, remote signals or barrier semaphores. Data moves between devices by JAX's collectives and lax.ppermute only.
A program may use at most 128 MiB of HBM per device.

```python
import math
import jax
import jax.numpy as jnp
import numpy as np
from jax import lax

D = 1024
HEADS = 16
HEAD_DIM = 64
FF = 2624
HD = 1024
SLOT = 1024
SEQS = 1
SLAB = 1024
NSEQ = 8
TOKENS = 8192
N_DP = 4
N_ROW = 2


def block_levels(key, extent, split, low, top_value):
    def one(position, blocks):
        draws = jax.random.uniform(jax.random.fold_in(jax.random.fold_in(key, 6), position), (blocks,), jnp.float32, low / len(split), top_value / len(split))
        return jnp.repeat(jnp.exp(draws), extent[position] // blocks).reshape((-1,) + (1,) * (len(extent) - position - 1))

    level = one(*split[0])
    for cut in split[1:]:
        level = level * one(*cut)
    return level


def split_up(amount, total, bound, slope):
    portions = [(1 << 20) // math.isqrt(grade ** slope) + 1 for grade in range(2, amount + 1)]
    rest, given = total - bound - (amount - 1), [1] * (amount - 1)
    while rest > 0:
        movable = [i for i in range(amount - 1) if given[i] < bound]
        mass, left = sum([portions[i] for i in movable]), rest
        for i in movable:
            extra = min(bound - given[i], max(1, left * portions[i] // mass), rest)
            given[i] = given[i] + extra
            rest = rest - extra
    return np.array([bound] + given)


def uneven(key, amount, total, most, slope):
    if amount == 2:
        one = jax.random.randint(key, (), max(1, total - most), min(most, total - 1) + 1)
        return jnp.stack([one, total - one])
    sizes = jnp.asarray(split_up(amount, total, most, slope), jnp.int32)
    twos = (amount - 1) // 2
    giver, taker = sizes[1:1 + 2 * twos:2], sizes[2:2 + 2 * twos:2]
    margin = jnp.minimum(giver - 1, most - taker)
    passed = jax.random.randint(jax.random.fold_in(key, 1), (twos,), 0, 1 << 20) % (margin + 1)
    sizes = sizes.at[1:1 + 2 * twos:2].set(giver - passed).at[2:2 + 2 * twos:2].set(taker + passed)
    return sizes[jax.random.permutation(jax.random.fold_in(key, 2), amount)]


def scatter_about(rng, extent, scale, bound, shards=(), kind=jnp.bfloat16):
    result = jax.random.normal(rng, extent, jnp.float32) * scale
    if len(shards) > 0:
        result = block_levels(rng, extent, shards, -0.22, 0.18) * result
    return jnp.clip(result, min=-bound, max=bound).astype(kind)


def setup_inputs(seed: int = 0) -> dict:
    seeds = jax.random.split(jax.random.key(seed), 11)
    return {
        "activations": scatter_about(seeds[0], (TOKENS, D), 1.0, 6.0, ((0, 32),)),
        "upstream_grad": scatter_about(seeds[1], (TOKENS, D), 1.0, 6.0, ((0, 32),)),
        "w_qkv": scatter_about(seeds[2], (D, 3, HD), D ** -0.5, 0.1875, ((0, 8), (2, 4))),
        "w_out_attn": scatter_about(seeds[3], (HD, D), (max(1, HD * 4 // SLAB)) ** -0.5, 3.0, ((0, 4), (1, 8))),
        "w_in": scatter_about(seeds[4], (D, 2, FF), D ** -0.5, 0.1875, ((0, 8), (2, 4))),
        "w_out_mlp": scatter_about(seeds[5], (FF, D), FF ** -0.5, 0.125, ((0, 4), (1, 8))),
        "gain_attn": jnp.clip(1.0 + 0.1 * jax.random.normal(seeds[6], (D,), jnp.float32), 0.5, 1.5),
        "gain_mlp": jnp.clip(1.0 + 0.1 * jax.random.normal(seeds[7], (D,), jnp.float32), 0.5, 1.5),
        "lengths": uneven(seeds[8], NSEQ, NSEQ * SLOT * 5 // 8, SLOT, 1).astype(jnp.int32),
        "seq_order": jax.random.permutation(seeds[9], NSEQ).astype(jnp.int32),
    }


HIGHEST_PRECISION = lax.Precision.HIGHEST
EPSILON = 1e-05
ROPE_BASE = 160000.0
NEG_LARGE = -1e+30

@jax.custom_vjp
def low(v):
    return lax.optimization_barrier(v.astype(jnp.bfloat16)).astype(jnp.float32)

@jax.custom_vjp
def low_back(v):
    return v

def low_keep(v):
    return (low(v), None)

def low_pass(kept, grad):
    return (grad,)

def back_keep(v):
    return (v, None)

def back_low(kept, grad):
    return (low(grad),)
low.defvjp(low_keep, low_pass)
low_back.defvjp(back_keep, back_low)

def layer_norm(inputs, gain):
    average = lax.optimization_barrier(jnp.mean(inputs, axis=-1, keepdims=True))
    centred = inputs - average
    variance = lax.optimization_barrier(jnp.mean(centred * centred, axis=-1, keepdims=True))
    return centred * lax.rsqrt(variance + EPSILON) * gain

def rotary_tables():
    halfway = HEAD_DIM // 2
    inverse = ROPE_BASE ** (-(jnp.arange(halfway).astype(jnp.float32) * 2.0) / HEAD_DIM)
    places = jnp.arange(SLOT).astype(jnp.float32)
    angles = places[:, None] * inverse[None, :]
    angles = jnp.concatenate([angles, angles], axis=1)
    return (jnp.cos(angles), jnp.sin(angles))

def rotate(inputs, cos_table, sin_table):
    halfway = inputs.shape[-1] // 2
    turned = jnp.concatenate([-inputs[..., halfway:], inputs[..., :halfway]], axis=-1)
    return inputs * cos_table[:, None, :] + turned * sin_table[:, None, :]

def slab_forward(params, inputs, slot_len):
    w_qkv, w_out_attn, w_in, w_out_mlp, gain_attn, gain_mlp = params
    places = jnp.arange(SLOT)
    key_valid = places[None, :] < slot_len[:, None]
    row_valid = key_valid.reshape(SLAB, 1)
    cos_table, sin_table = rotary_tables()
    normed_one = low(layer_norm(inputs, gain_attn))
    projected = low_back(jnp.einsum('td,dkh->tkh', normed_one, w_qkv, precision=HIGHEST_PRECISION))
    projected = projected.reshape(SEQS, SLOT, 3, HEADS, HEAD_DIM)
    queries = low(rotate(projected[:, :, 0], cos_table, sin_table))
    key_rows = low(rotate(projected[:, :, 1], cos_table, sin_table))
    value_rows = low(projected[:, :, 2])
    scores = jnp.einsum('sqhd,skhd->shqk', queries, key_rows, precision=HIGHEST_PRECISION)
    scores = low_back(scores * HEAD_DIM ** (-0.5))
    scores = jnp.where(key_valid[:, None, None, :], scores, NEG_LARGE)
    prob_low = low(jax.nn.softmax(scores, axis=-1))
    attended = jnp.einsum('shqk,skhd->sqhd', prob_low, value_rows, precision=HIGHEST_PRECISION)
    attended = low_back(low(attended.reshape(SLAB, HD)))
    branch = low_back(jnp.dot(attended, w_out_attn, precision=HIGHEST_PRECISION))
    hidden = inputs + branch
    normed_two = low(layer_norm(hidden, gain_mlp))
    expanded = low_back(jnp.einsum('td,dkf->tkf', normed_two, w_in, precision=HIGHEST_PRECISION))
    gated = low(jax.nn.gelu(expanded[:, 0], approximate=False) * expanded[:, 1])
    mlp_out = low_back(jnp.dot(gated, w_out_mlp, precision=HIGHEST_PRECISION))
    return jnp.where(row_valid, hidden + mlp_out, 0.0)

def reference(activations, upstream_grad, w_qkv, w_out_attn, w_in, w_out_mlp, gain_attn, gain_mlp, lengths, seq_order):
    slab_count = N_DP * N_ROW
    slot_len = jnp.take(lengths, seq_order).reshape(slab_count, SEQS)
    params = (w_qkv.astype(jnp.float32), w_out_attn.astype(jnp.float32), w_in.astype(jnp.float32), w_out_mlp.astype(jnp.float32), gain_attn.astype(jnp.float32), gain_mlp.astype(jnp.float32))
    inputs = activations.astype(jnp.float32).reshape(slab_count, SLAB, D)
    upstream = upstream_grad.astype(jnp.float32).reshape(slab_count, SLAB, D)

    def forward(weights, stacked):

        def scan_step(carry, item):
            return (carry, jax.checkpoint(slab_forward)(weights, item[0], item[1]))
        _, outputs = lax.scan(scan_step, None, (stacked, slot_len))
        return outputs
    outputs, pullback = jax.vjp(forward, params, inputs)
    grad_params, grad_inputs = pullback(upstream)
    return (outputs.reshape(TOKENS, D).astype(jnp.bfloat16), grad_inputs.reshape(TOKENS, D).astype(jnp.bfloat16), grad_params[0], grad_params[1], grad_params[2], grad_params[3], grad_params[4], grad_params[5])
```

```python
import jax
import jax.numpy as jnp
from jax import lax
from jax.sharding import PartitionSpec as P

HEAD_DIM = 64
EPSILON = 1e-05
ROPE_BASE = 160000.0
NEG_LARGE = -1e30
BF = jnp.bfloat16
F32 = jnp.float32


def exchange(value, axis, bit):
    count = lax.axis_size(axis)
    return lax.ppermute(value, axis, [(i, i ^ bit) for i in range(count)])


def bits_of(axis):
    count = lax.axis_size(axis)
    bit = count // 2
    found = []
    while bit:
        found.append((axis, bit))
        bit //= 2
    return found


def weight_stages():
    return bits_of("dp") + bits_of("row")


def source_shard(relative, stages):
    place = {"dp": lax.axis_index("dp"), "row": lax.axis_index("row")}
    for step, (axis, bit) in enumerate(stages):
        if (relative >> step) & 1:
            place[axis] = place[axis] ^ bit
    return place["dp"] * lax.axis_size("row") + place["row"]


def relative_place(shard, stages):
    rows = lax.axis_size("row")
    apart = {
        "dp": lax.axis_index("dp") ^ (shard // rows),
        "row": lax.axis_index("row") ^ (shard % rows),
    }
    total = 0
    for step, (axis, bit) in enumerate(stages):
        total = total + jnp.where((apart[axis] & bit) != 0, 1 << step, 0)
    return total


def take_blocks(value, places, width):
    return jnp.concatenate(
        [lax.dynamic_slice_in_dim(value, p * width, width, value.ndim - 1) for p in places], -1
    )


def weight_gather(block, stages, dim):
    for axis, bit in stages:
        block = jnp.concatenate([block, exchange(block, axis, bit)], dim)
    return block


def weight_scatter(grad, stages, dim):
    for axis, bit in reversed(stages):
        half = grad.shape[dim] // 2
        keep = lax.slice_in_dim(grad, 0, half, axis=dim)
        send = lax.slice_in_dim(grad, half, 2 * half, axis=dim)
        grad = keep + exchange(send.astype(BF), axis, bit).astype(F32)
    return grad


def slab_gather(own):
    far = exchange(own, "col", 2)
    near = exchange(own, "col", 1)
    both = exchange(far, "col", 1)
    return jnp.concatenate([own, near, far, both], 0)


def slab_scatter(left, right, right_dim):
    part = contract(left, right, 1, right_dim)
    rows = part.shape[0] // 4
    part = part.reshape(2, 2, rows, part.shape[1])
    paired = part[:, 0] + exchange(part[:, 1].astype(BF), "col", 1).astype(F32)
    return paired[0] + exchange(paired[1].astype(BF), "col", 2).astype(F32)


def layer_norm(inputs, gain):
    average = jnp.mean(inputs, axis=-1, keepdims=True)
    centred = inputs - average
    variance = jnp.mean(centred * centred, axis=-1, keepdims=True)
    return centred * lax.rsqrt(variance + EPSILON) * gain


def gelu_gate(first, second):
    return jax.nn.gelu(first, approximate=False) * second


def rotary_tables(places):
    halfway = HEAD_DIM // 2
    inverse = ROPE_BASE ** (-(jnp.arange(halfway).astype(F32) * 2.0) / HEAD_DIM)
    angles = places.astype(F32)[:, None] * inverse[None, :]
    angles = jnp.concatenate([angles, angles], axis=1)
    return (jnp.cos(angles), jnp.sin(angles))


def rotate(inputs, cos_table, sin_table):
    halfway = inputs.shape[-1] // 2
    turned = jnp.concatenate([-inputs[..., halfway:], inputs[..., :halfway]], axis=-1)
    return inputs * cos_table[:, None, :] + turned * sin_table[:, None, :]


def rotate_back(grads, cos_table, sin_table):
    halfway = grads.shape[-1] // 2
    scaled = grads * sin_table[:, None, :]
    turned = jnp.concatenate([scaled[..., halfway:], -scaled[..., :halfway]], axis=-1)
    return grads * cos_table[:, None, :] + turned


def contract(left, right, left_dim, right_dim):
    return lax.dot_general(
        left, right, (((left_dim,), (right_dim,)), ((), ())), preferred_element_type=F32
    )


def attention_forward(queries, key_rows, value_rows, key_valid, score_scale):
    scores = jnp.einsum("qhd,khd->hqk", queries, key_rows, preferred_element_type=F32)
    scores = jnp.where(key_valid[None, None, :], scores * score_scale, NEG_LARGE)
    row_max = jnp.max(scores, axis=-1, keepdims=True)
    raised = jnp.exp(scores - row_max)
    row_total = jnp.sum(raised, axis=-1, keepdims=True)
    prob_low = (raised / row_total).astype(BF)
    output = jnp.einsum("hqk,khd->qhd", prob_low, value_rows, preferred_element_type=F32)
    return (output.astype(BF), prob_low)


def attention_backward(queries, key_rows, value_rows, grad_attended, prob_low, score_scale):
    probs = prob_low.astype(F32)
    grad_probs = jnp.einsum("qhd,khd->hqk", grad_attended, value_rows, preferred_element_type=F32)
    weighted = jnp.sum(probs * grad_probs, axis=-1, keepdims=True)
    grad_scores = (probs * (grad_probs - weighted)).astype(BF)
    grad_q = jnp.einsum("hqk,khd->qhd", grad_scores, key_rows, preferred_element_type=F32)
    grad_k = jnp.einsum("hqk,qhd->khd", grad_scores, queries, preferred_element_type=F32)
    grad_v = jnp.einsum("hqk,qhd->khd", prob_low, grad_attended, preferred_element_type=F32)
    return (grad_q * score_scale, grad_k * score_scale, grad_v)


def per_device(
    activations,
    upstream_grad,
    w_qkv,
    w_out_attn,
    w_in,
    w_out_mlp,
    gain_attn,
    gain_mlp,
    lengths,
    seq_order,
):
    own_rows, width = activations.shape
    slab_rows = own_rows * 4
    stages = weight_stages()
    shard_count = 1 << len(stages)
    shard_width = width // shard_count
    score_scale = HEAD_DIM ** (-0.5)
    row_count = lax.axis_size("row")
    slab_index = lax.axis_index("dp") * row_count + lax.axis_index("row")
    col_index = lax.axis_index("col")
    slab_ids = jnp.arange(seq_order.shape[0])
    seq_id = jnp.sum(jnp.where(slab_ids == slab_index, seq_order, 0))
    slot_len = jnp.sum(jnp.where(slab_ids == seq_id, lengths, 0))
    places = ((col_index ^ jnp.arange(4))[:, None] * own_rows + jnp.arange(own_rows)).reshape(-1)
    key_valid = places < slot_len
    own_valid = key_valid[:own_rows, None]
    cos_table, sin_table = rotary_tables(places)

    order_in = [source_shard(j, stages) for j in range(shard_count)]
    order_out = [relative_place(s, stages) for s in range(shard_count)]
    inputs = take_blocks(activations, order_in, shard_width).astype(F32)
    upstream = take_blocks(upstream_grad, order_in, shard_width)
    gain_one = take_blocks(gain_attn[None], order_in, shard_width)[0]
    gain_two = take_blocks(gain_mlp[None], order_in, shard_width)[0]

    full_qkv = weight_gather(w_qkv.reshape(shard_width, -1), stages, 0)
    full_attn = weight_gather(w_out_attn, stages, 1)
    full_in = weight_gather(w_in.reshape(shard_width, -1), stages, 0)
    full_mlp = weight_gather(w_out_mlp, stages, 1)
    width_qkv = full_qkv.shape[1] // 3
    width_ff = full_in.shape[1] // 2
    heads_local = width_qkv // HEAD_DIM

    norm_one, norm_one_back = jax.vjp(layer_norm, inputs, gain_one)
    normed_one = slab_gather(norm_one.astype(BF))
    grad_out = jnp.where(own_valid, upstream.astype(F32), 0.0)
    grad_out_low = slab_gather(grad_out.astype(BF))
    projected = contract(normed_one, full_qkv, 1, 0)
    projected = projected.reshape(slab_rows, 3, heads_local, HEAD_DIM)
    queries = rotate(projected[:, 0], cos_table, sin_table).astype(BF)
    key_rows = rotate(projected[:, 1], cos_table, sin_table).astype(BF)
    value_rows = projected[:, 2].astype(BF)
    attended, prob_low = attention_forward(queries, key_rows, value_rows, key_valid, score_scale)
    attended = attended.reshape(slab_rows, width_qkv)
    hidden = inputs + slab_scatter(attended, full_attn, 0)
    norm_two, norm_two_back = jax.vjp(layer_norm, hidden, gain_two)
    normed_two = slab_gather(norm_two.astype(BF))
    expanded = contract(normed_two, full_in, 1, 0).reshape(slab_rows, 2, width_ff)
    gated, gate_back = jax.vjp(gelu_gate, expanded[:, 0], expanded[:, 1])
    gated_low = gated.astype(BF)
    mlp_out = slab_scatter(gated_low, full_mlp, 0)
    block_out = jnp.where(own_valid, hidden + mlp_out, 0.0).astype(BF)

    grad_gated = contract(grad_out_low, full_mlp, 1, 1)
    grad_first, grad_second = gate_back(grad_gated)
    grad_expanded = jnp.stack([grad_first, grad_second], axis=1).astype(BF)
    grad_expanded = grad_expanded.reshape(slab_rows, 2 * width_ff)
    grad_normed_two = slab_scatter(grad_expanded, full_in, 1)
    hidden_part, grad_gain_two = norm_two_back(grad_normed_two)
    grad_hidden = grad_out + hidden_part
    grad_hidden_low = slab_gather(grad_hidden.astype(BF))
    grad_w_out_mlp = weight_scatter(contract(gated_low, grad_out_low, 0, 0), stages, 1)
    grad_w_in = weight_scatter(contract(normed_two, grad_expanded, 0, 0), stages, 0)
    grad_w_out_attn = weight_scatter(contract(attended, grad_hidden_low, 0, 0), stages, 1)
    grad_attended = contract(grad_hidden_low, full_attn, 1, 1).astype(BF)
    grad_attended = grad_attended.reshape(slab_rows, heads_local, HEAD_DIM)
    grad_q, grad_k, grad_v = attention_backward(
        queries, key_rows, value_rows, grad_attended, prob_low, score_scale
    )
    grad_projected = jnp.stack(
        [
            rotate_back(grad_q, cos_table, sin_table),
            rotate_back(grad_k, cos_table, sin_table),
            grad_v,
        ],
        axis=1,
    )
    grad_projected = grad_projected.astype(BF).reshape(slab_rows, 3 * width_qkv)
    grad_w_qkv = weight_scatter(contract(normed_one, grad_projected, 0, 0), stages, 0)
    grad_normed_one = slab_scatter(grad_projected, full_qkv, 1)
    input_part, grad_gain_one = norm_one_back(grad_normed_one)
    grad_input = (grad_hidden + input_part).astype(BF)

    gains = take_blocks(jnp.stack([grad_gain_one, grad_gain_two]), order_out, shard_width)
    for axis, bit in bits_of("col") + stages:
        gains = gains + exchange(gains, axis, bit)
    return (
        take_blocks(block_out, order_out, shard_width),
        take_blocks(grad_input, order_out, shard_width),
        grad_w_qkv.reshape(w_qkv.shape),
        grad_w_out_attn,
        grad_w_in.reshape(w_in.shape),
        grad_w_out_mlp,
        gains[0],
        gains[1],
    )


def solution(mesh):
    rows = P(("dp", "row", "col"), None)
    tall = P(("dp", "row"), None, "col")
    wide = P("col", ("dp", "row"))
    return jax.shard_map(
        per_device,
        mesh=mesh,
        in_specs=(rows, rows, tall, wide, tall, wide, P(), P(), P(), P()),
        out_specs=(rows, rows, tall, wide, tall, wide, P(), P()),
        check_vma=False,
    )
```

```python
import math
import jax
import jax.numpy as jnp
from jax import lax
from jax.experimental import pallas as pl
from jax.experimental.pallas import tpu as pltpu
from jax.sharding import PartitionSpec as P

HEAD_DIM = 64
PAIR = 2 * HEAD_DIM
LANES = 128
EPSILON = 1e-05
ROPE_BASE = 160000.0
NEG_LARGE = -1e30
BF = jnp.bfloat16
F32 = jnp.float32
VMEM_LIMIT = 56 * 2**20


def exchange(value, axis, bit):
    count = lax.axis_size(axis)
    return lax.ppermute(value, axis, [(i, i ^ bit) for i in range(count)])


def bits_of(axis):
    bit = lax.axis_size(axis) // 2
    found = []
    while bit:
        found.append((axis, bit))
        bit //= 2
    return found


def own_bit(axis, bit):
    return (lax.axis_index(axis) // bit) % 2


def source_shards(stages):
    rows = lax.axis_size("row")
    found = []
    for place in range(1 << len(stages)):
        at = {"dp": lax.axis_index("dp"), "row": lax.axis_index("row")}
        for step, (axis, bit) in enumerate(stages):
            if (place >> step) & 1:
                at[axis] = at[axis] ^ bit
        found.append(at["dp"] * rows + at["row"])
    return jnp.stack(found).astype(jnp.int32)


def gather_blocks(block, stages):
    pieces = [block[None]]
    for axis, bit in stages[:-1]:
        whole = jnp.concatenate(pieces, 0) if len(pieces) > 1 else pieces[0]
        pieces.append(exchange(whole, axis, bit))
    return pieces + [exchange(piece, *stages[-1]) for piece in pieces]


def scatter_rest(keep, got, order, bits):
    left = [b for b in bits if b != order[0]]
    tail = keep.shape[1:]
    keep = keep.reshape((2,) * len(left) + tail)
    got = got.reshape((2,) * len(left) + tail)
    for axis, bit in order[1:]:
        dim, mine = left.index((axis, bit)), own_bit(axis, bit)
        pick = lambda value, which: lax.dynamic_index_in_dim(value, which, dim, keepdims=False)
        send = pick(keep, 1 - mine) + pick(got, 1 - mine).astype(F32)
        recv = exchange(send.astype(BF), axis, bit)
        keep, got = pick(keep, mine) + pick(got, mine).astype(F32), recv
        left.pop(dim)
    return keep + got.astype(F32)


def first_tables(order, bits):
    axis, bit = order[0]
    position = len(bits) - 1 - bits.index(order[0])
    mine = own_bit(axis, bit)
    low = (1 << position) - 1
    base = [((i & ~low) << 1) | (i & low) for i in range(1 << (len(bits) - 1))]
    base = jnp.array(base, jnp.int32)
    return base + (mine << position).astype(jnp.int32), base + ((1 - mine) << position).astype(jnp.int32)


def params(dims):
    return pltpu.CompilerParams(
        dimension_semantics=("arbitrary",) * dims, vmem_limit_bytes=VMEM_LIMIT
    )


def cost(flops, moved, raised=0):
    return pl.CostEstimate(flops=flops, bytes_accessed=moved, transcendentals=raised)


def dot(left, right, left_dim, right_dim):
    return lax.dot_general(
        left, right, (((left_dim,), (right_dim,)), ((), ())), preferred_element_type=F32
    )


def turn(value, cos_table, sin_table):
    width = value.shape[1]
    repeats = width // cos_table.shape[1]
    if repeats > 1:
        cos_table = jnp.concatenate([cos_table] * repeats, 1)
        sin_table = jnp.concatenate([sin_table] * repeats, 1)
    half = HEAD_DIM // 2
    lane = lax.broadcasted_iota(jnp.int32, value.shape, 1)
    swapped = jnp.where(
        lane % HEAD_DIM < half, pltpu.roll(value, width - half, 1), pltpu.roll(value, half, 1)
    )
    return value * cos_table + swapped * sin_table


def ordered(pieces, table, dim):
    width = pieces[0].shape[dim]
    if width % LANES == 0:
        return pieces, table
    blocks = jnp.concatenate(pieces, 0)
    blocks = jnp.zeros_like(blocks).at[table].set(blocks)
    blocks = jnp.moveaxis(blocks, 0, dim - 1)
    shape = blocks.shape[: dim - 1] + (-1,) + blocks.shape[dim + 1 :]
    return [blocks.reshape(shape)[None]], jnp.zeros((1,), jnp.int32)


def block_starts(refs, table_ref, dim):
    place = 0
    for ref in refs:
        width = ref.shape[dim]
        for j in range(ref.shape[0]):
            yield ref.at[j], pl.ds(pl.multiple_of(table_ref[place] * width, LANES), width)
            place += 1


def whole_spec(value):
    zeros = (0,) * value.ndim
    return pl.BlockSpec(value.shape, lambda *_: zeros)


def project_kernel(counts, table_a, table_b, *refs):
    row_refs, refs = refs[:4], refs[4:]
    a_refs, refs = refs[: counts[0]], refs[counts[0] :]
    b_refs, refs = refs[: counts[1]], refs[counts[1] :]
    cos_ref, sin_ref, q_ref, k_ref, v_ref, weight_ref = refs
    for piece, where in block_starts(a_refs, table_a, 2):
        weight_ref[:, where, :LANES] = piece[...]
    for piece, where in block_starts(b_refs, table_b, 2):
        weight_ref[:, where, LANES:] = piece[...]
    size = row_refs[0].shape[0]
    for i, row_ref in enumerate(row_refs):
        part = slice(i * size, (i + 1) * size)
        rows, cos_table, sin_table = row_ref[...], cos_ref[part], sin_ref[part]
        queries = turn(dot(rows, weight_ref[0], 1, 0), cos_table, sin_table) * (HEAD_DIM**-0.5)
        q_ref[part] = queries.astype(BF)
        k_ref[part] = turn(dot(rows, weight_ref[1], 1, 0), cos_table, sin_table).astype(BF)
        v_ref[part] = dot(rows, weight_ref[2], 1, 0).astype(BF)


def project(rows, pieces_a, table_a, pieces_b, table_b, cos_table, sin_table):
    pieces_a, table_a = ordered(pieces_a, table_a, 2)
    pieces_b, table_b = ordered(pieces_b, table_b, 2)
    count, depth = 4 * rows[0].shape[0], rows[0].shape[1]
    width = 2 * pieces_a[0].shape[3]
    args = [*rows, *pieces_a, *pieces_b, cos_table, sin_table]
    counts = (len(pieces_a), len(pieces_b))
    out = [jax.ShapeDtypeStruct((count, width), BF)] * 3
    out.append(jax.ShapeDtypeStruct((3, depth, width), BF))
    return pl.pallas_call(
        lambda *refs: project_kernel(counts, *refs),
        grid_spec=pltpu.PrefetchScalarGridSpec(
            num_scalar_prefetch=2,
            grid=(1,),
            in_specs=[whole_spec(a) for a in args],
            out_specs=[whole_spec(o) for o in out],
        ),
        out_shape=out,
        compiler_params=params(1),
        cost_estimate=cost(6 * count * depth * width, 8 * 2**20),
        name="project",
    )(table_a, table_b, *args)


def attend_kernel(bias_ref, q_ref, k_ref, v_ref, out_ref, prob_ref):
    queries, key_rows, values = q_ref[...], k_ref[...], v_ref[...]
    bias = bias_ref[...]
    q_lane = lax.broadcasted_iota(jnp.int32, queries.shape, 1)
    k_lane = lax.broadcasted_iota(jnp.int32, key_rows.shape, 1)
    values_t = values.T
    outs = []
    for head in range(2):
        low, spare = head * HEAD_DIM, (1 - head) * HEAD_DIM
        one = jnp.where(q_lane == spare, 1, 0).astype(BF)
        q_own = jnp.where(q_lane // HEAD_DIM == head, queries, one)
        k_own = jnp.where(k_lane == spare, bias, key_rows)
        scores = dot(k_own, q_own, 1, 1)
        top = jnp.max(scores, axis=0, keepdims=True)
        raised = jnp.exp(scores - top)
        total = jnp.sum(raised, axis=0, keepdims=True)
        prob = (raised * (1.0 / total)).astype(BF)
        prob_ref[head] = prob
        outs.append(dot(values_t[low : low + HEAD_DIM], prob, 1, 0))
    out_ref[...] = jnp.concatenate(outs, 0).T.astype(BF)


def attend(bias, queries, key_rows, values, half, block=512):
    keys, width = queries.shape
    count = keys // 2
    pairs, steps = width // PAIR, count // block
    whole = pl.BlockSpec((keys, PAIR), lambda p, i: (0, p))
    return pl.pallas_call(
        attend_kernel,
        grid=(pairs, steps),
        in_specs=[
            pl.BlockSpec((keys, PAIR), lambda p, i: (0, 0)),
            pl.BlockSpec((block, PAIR), lambda p, i: (half * steps + i, p)),
            whole,
            whole,
        ],
        out_specs=[
            pl.BlockSpec((block, PAIR), lambda p, i: (i, p)),
            pl.BlockSpec((2, keys, block), lambda p, i: (p, 0, i)),
        ],
        out_shape=[
            jax.ShapeDtypeStruct((count, width), BF),
            jax.ShapeDtypeStruct((2 * pairs, keys, count), BF),
        ],
        compiler_params=params(2),
        cost_estimate=cost(16 * keys * count * width, 8 * 2**20, 2 * pairs * keys * count),
        name="attend",
    )(bias, queries, key_rows, values)


def attend_back_kernel(last, *refs):
    prob_ref, gh_ref, gh_next_ref, w_ref, out_ref, q_ref, k_ref, v_ref, cosq_ref, sinq_ref = refs[:10]
    if last:
        cos_ref, sin_ref, ksum_ref, vsum_ref, gq_ref, gk_ref, gv_ref = refs[10:]
    else:
        gq_ref, gk_ref, gv_ref = refs[10:]
    weight = w_ref[...]
    grad = jnp.concatenate([dot(gh_ref[...], weight, 1, 1), dot(gh_next_ref[...], weight, 1, 1)], 0)
    grad = grad.astype(BF)
    queries, key_rows, values = q_ref[...], k_ref[...], v_ref[...]
    product_t = (grad.astype(F32) * out_ref[...].astype(F32)).T
    v_lane = lax.broadcasted_iota(jnp.int32, values.shape, 1)
    keys_t = key_rows.T
    k_parts, v_parts, q_parts = [], [], []
    for head in range(2):
        low = head * HEAD_DIM
        prob = prob_ref[head]
        weighted = jnp.sum(product_t[low : low + HEAD_DIM], axis=0, keepdims=True)
        v_own = jnp.where(v_lane // HEAD_DIM == head, values, jnp.zeros_like(values))
        grad_prob = dot(v_own, grad, 1, 1)
        grad_score = (prob.astype(F32) * (grad_prob - weighted)).astype(BF)
        v_parts.append(dot(prob, grad, 1, 0))
        k_parts.append(dot(grad_score, queries, 1, 0))
        q_parts.append(dot(keys_t[low : low + HEAD_DIM], grad_score, 1, 0))
    grad_q = jnp.concatenate(q_parts, 0).T * (HEAD_DIM**-0.5)
    gq_ref[...] = turn(grad_q, cosq_ref[...], -sinq_ref[...]).astype(BF)
    own = v_lane < HEAD_DIM
    k_part = jnp.where(own, k_parts[0], k_parts[1])
    v_part = jnp.where(own, v_parts[0], v_parts[1])
    if last:
        gk_ref[...] = turn(k_part + ksum_ref[...], cos_ref[...], -sin_ref[...]).astype(BF)
        gv_ref[...] = (v_part + vsum_ref[...]).astype(BF)
    else:
        gk_ref[...] = k_part
        gv_ref[...] = v_part


def attend_back(prob, grads, weight, out, queries, key_rows, values, cos_table, sin_table, half, sums=None):
    keys, width = queries.shape
    count = keys // 2
    pairs = width // PAIR
    last = sums is not None
    whole = pl.BlockSpec((keys, PAIR), lambda p: (0, p))
    part = pl.BlockSpec((count, PAIR), lambda p: (0, p))
    table = pl.BlockSpec((keys, PAIR), lambda p: (0, 0))
    table_part = pl.BlockSpec((count, PAIR), lambda p: (half, 0))
    q_part = pl.BlockSpec((count, PAIR), lambda p: (half, p))
    prob_spec = pl.BlockSpec((2, keys, count), lambda p: (p, 0, 0))
    in_specs = [prob_spec, whole_spec(grads[0]), whole_spec(grads[1])]
    in_specs.append(pl.BlockSpec((PAIR, weight.shape[1]), lambda p: (p, 0)))
    in_specs += [part, q_part, whole, whole, table_part, table_part]
    args = [prob, *grads, weight, out, queries, key_rows, values, cos_table, sin_table]
    if last:
        in_specs += [table, table, whole, whole]
        args += [cos_table, sin_table, *sums]
    sum_type = BF if last else F32
    return pl.pallas_call(
        lambda *refs: attend_back_kernel(last, *refs),
        grid=(pairs,),
        in_specs=in_specs,
        out_specs=[part, whole, whole],
        out_shape=[
            jax.ShapeDtypeStruct((count, width), BF),
            jax.ShapeDtypeStruct((keys, width), sum_type),
            jax.ShapeDtypeStruct((keys, width), sum_type),
        ],
        compiler_params=params(1),
        cost_estimate=cost(32 * keys * count * width, 8 * 2**20),
        name="attend_back",
    )(*args)


def branch_kernel(table_ref, att_ref, *refs):
    keep_ref, send_ref, weight_ref = refs[-3:]
    for piece, where in block_starts(refs[:-3], table_ref, 2):
        weight_ref[:, where] = piece[...]
    rows = keep_ref.shape[0]
    weight = weight_ref[...]
    keep_ref[...] = dot(att_ref[:rows], weight, 1, 0).astype(BF)
    send_ref[...] = dot(att_ref[rows:], weight, 1, 0).astype(BF)


def branch(attended, pieces, table):
    pieces, table = ordered(pieces, table, 2)
    count, width = attended.shape
    depth = sum(p.shape[0] for p in pieces) * pieces[0].shape[2]
    half = jax.ShapeDtypeStruct((count // 2, depth), BF)
    out = [half, half, jax.ShapeDtypeStruct((width, depth), BF)]
    return pl.pallas_call(
        branch_kernel,
        grid_spec=pltpu.PrefetchScalarGridSpec(
            num_scalar_prefetch=1,
            grid=(1,),
            in_specs=[whole_spec(a) for a in (attended, *pieces)],
            out_specs=[whole_spec(o) for o in out],
        ),
        out_shape=out,
        compiler_params=params(1),
        cost_estimate=cost(2 * count * depth * width, 4 * 2**20),
        name="branch",
    )(table, attended, *pieces)


def feed_kernel(counts, table_ref, *refs):
    row_refs, grad_refs, refs = refs[:2], refs[2:4], refs[4:]
    in_refs, refs = refs[: counts[0]], refs[counts[0] :]
    out_refs, refs = refs[: counts[1]], refs[counts[1] :]
    mlp_refs, refs = refs[:2], refs[2:]
    gated_ref, first_ref, second_ref, refs = refs[0], refs[1], refs[2], refs[3:]
    gnorm_refs, (win_ref, wout_ref) = refs[:2], refs[2:]
    for piece, where in block_starts(in_refs, table_ref, 2):
        win_ref[:, where] = piece[...]
    for piece, where in block_starts(out_refs, table_ref, 2):
        wout_ref[:, where] = piece[...]
    units, size = gated_ref.shape[1], row_refs[0].shape[0]
    for i in range(2):
        part = slice(i * size, (i + 1) * size)
        rows, grad = row_refs[i][...], grad_refs[i][...]
        first = dot(rows, win_ref[:units], 1, 1)
        second = dot(rows, win_ref[units:], 1, 1)
        grad_gated = dot(grad, wout_ref[...], 1, 1)
        normal = 0.5 * (1.0 + lax.erf(first * (0.5**0.5)))
        gelu = first * normal
        density = jnp.exp(-0.5 * first * first) * ((2.0 * math.pi) ** -0.5)
        gated = (gelu * second).astype(BF)
        gated_ref[part] = gated
        grad_first = (grad_gated * second * (normal + first * density)).astype(BF)
        grad_second = (grad_gated * gelu).astype(BF)
        first_ref[part] = grad_first
        second_ref[part] = grad_second
        gnorm = dot(grad_first, win_ref[:units], 1, 0) + dot(grad_second, win_ref[units:], 1, 0)
        gnorm_refs[i][...] = gnorm.astype(BF)
        mlp_refs[i][...] = dot(gated, wout_ref[...], 1, 0).astype(BF)


def feed(rows, grads, in_pieces, out_pieces, table):
    in_pieces, in_table = ordered(in_pieces, table, 2)
    out_pieces, in_table = ordered(out_pieces, table, 2)
    count, depth = 2 * rows[0].shape[0], rows[0].shape[1]
    units = out_pieces[0].shape[1]
    half = jax.ShapeDtypeStruct((count // 2, depth), BF)
    hidden = jax.ShapeDtypeStruct((count, units), BF)
    args = [*rows, *grads, *in_pieces, *out_pieces]
    counts = (len(in_pieces), len(out_pieces))
    out = [half, half, hidden, hidden, hidden, half, half]
    return pl.pallas_call(
        lambda *refs: feed_kernel(counts, *refs),
        grid_spec=pltpu.PrefetchScalarGridSpec(
            num_scalar_prefetch=1,
            grid=(1,),
            in_specs=[whole_spec(a) for a in args],
            out_specs=[whole_spec(o) for o in out],
            scratch_shapes=[pltpu.VMEM((2 * units, depth), BF), pltpu.VMEM((units, depth), BF)],
        ),
        out_shape=out,
        compiler_params=params(1),
        cost_estimate=cost(12 * count * depth * units, 12 * 2**20, 2 * count * units),
        name="feed",
    )(in_table, *args)


def wide_grad_kernel(counts, kept_ref, sent_ref, *refs):
    keep_ref, send_ref = refs[-2:]
    width, at, row = keep_ref.shape[1], 0, 0
    rights = {}
    for left_count, right_key, right_count in counts:
        lefts = refs[at : at + left_count]
        at += left_count
        if right_count:
            kept, sent = refs[at : at + right_count], refs[at + right_count : at + 2 * right_count]
            at += 2 * right_count
            both = [jnp.concatenate([k[...], s[...]], 1) for k, s in zip(kept, sent)]
            rights[right_key] = jnp.concatenate(both, 0)
        right = rights[right_key]
        total, start = 0.0, 0
        for left in lefts:
            size = left.shape[0]
            total = total + dot(left[...], right[start : start + size], 0, 0)
            start += size
        keep_ref[row : row + total.shape[0]] = total[:, :width]
        send_ref[row : row + total.shape[0]] = total[:, width:].astype(BF)
        row += total.shape[0]


def wide_grad(groups, order, bits, width):
    kept, sent = first_tables(order, bits)
    steps = kept.shape[0]
    rows = sum(lefts[0].shape[1] for lefts, _ in groups)
    if width % LANES:
        total = [dot(jnp.concatenate(a, 0), jnp.concatenate(b, 0), 0, 0) for a, b in groups]
        blocks = jnp.concatenate(total, 0).reshape(rows, 2 * steps, width)
        blocks = jnp.moveaxis(blocks, 1, 0)
        return blocks[kept], blocks[sent].astype(BF)
    in_specs, args, counts, flops, seen = [], [], [], 0, {}
    for lefts, rights in groups:
        in_specs += [whole_spec(a) for a in lefts]
        args += lefts
        known = id(rights) in seen
        key = seen.setdefault(id(rights), len(seen))
        counts.append((len(lefts), key, 0 if known else len(rights)))
        if not known:
            shape = (rights[0].shape[0], width)
            in_specs += [pl.BlockSpec(shape, lambda i, k, s: (0, k[i]))] * len(rights)
            in_specs += [pl.BlockSpec(shape, lambda i, k, s: (0, s[i]))] * len(rights)
            args += [*rights, *rights]
        flops += 2 * sum(a.size for a in lefts) * rights[0].shape[1]
    out_spec = pl.BlockSpec((pl.Squeezed(), rows, width), lambda i, k, s: (i, 0, 0))
    return pl.pallas_call(
        lambda *refs: wide_grad_kernel(counts, *refs),
        grid_spec=pltpu.PrefetchScalarGridSpec(
            num_scalar_prefetch=2,
            grid=(steps,),
            in_specs=in_specs,
            out_specs=[out_spec, out_spec],
        ),
        out_shape=[
            jax.ShapeDtypeStruct((steps, rows, width), F32),
            jax.ShapeDtypeStruct((steps, rows, width), BF),
        ],
        compiler_params=params(1),
        cost_estimate=cost(flops, 16 * 2**20),
        name="wide_grad",
    )(kept, sent, *args)


def tall_grad_kernel(kept_ref, sent_ref, *refs):
    kept, sent, grad_refs, (keep_ref, send_ref) = refs[:4], refs[4:8], refs[8:12], refs[12:]
    left = jnp.concatenate([jnp.concatenate([k[...], s[...]], 1) for k, s in zip(kept, sent)], 0)
    width = keep_ref.shape[1]
    grad_q = jnp.concatenate([grad_refs[0][...], grad_refs[1][...]], 0)
    for part, grads in enumerate((grad_q, grad_refs[2][...], grad_refs[3][...])):
        total = dot(left, grads, 0, 0)
        keep_ref[part] = total[:width]
        send_ref[part] = total[width:].astype(BF)


def tall_grad(rows, grads, lanes, order, bits, width):
    kept, sent = first_tables(order, bits)
    steps, size = kept.shape[0], rows[0].shape[0]
    if width % LANES:
        cut = [g[:, lanes * LANES : (lanes + 1) * LANES] for g in grads]
        cut = [jnp.concatenate(cut[:2], 0), *cut[2:]]
        total = jnp.stack([dot(jnp.concatenate(rows, 0), g, 0, 0) for g in cut])
        blocks = jnp.moveaxis(total.reshape(3, 2 * steps, width, LANES), 1, 0)
        return blocks[kept], blocks[sent].astype(BF)
    out_spec = pl.BlockSpec((pl.Squeezed(), 3, width, LANES), lambda i, k, s: (i, 0, 0, 0))
    grad_specs = [pl.BlockSpec((g.shape[0], LANES), lambda i, k, s: (0, lanes)) for g in grads]
    return pl.pallas_call(
        tall_grad_kernel,
        grid_spec=pltpu.PrefetchScalarGridSpec(
            num_scalar_prefetch=2,
            grid=(steps,),
            in_specs=[pl.BlockSpec((size, width), lambda i, k, s: (0, k[i]))] * 4
            + [pl.BlockSpec((size, width), lambda i, k, s: (0, s[i]))] * 4
            + grad_specs,
            out_specs=[out_spec, out_spec],
        ),
        out_shape=[
            jax.ShapeDtypeStruct((steps, 3, width, LANES), F32),
            jax.ShapeDtypeStruct((steps, 3, width, LANES), BF),
        ],
        compiler_params=params(1),
        cost_estimate=cost(48 * steps * width * size * LANES, 8 * 2**20),
        name="tall_grad",
    )(kept, sent, *rows, *rows, *grads)


def project_back_kernel(gq_ref, gk_ref, gv_ref, weight_ref, n_ref, n_next_ref, keep_ref, send_ref, gain_ref):
    total = dot(gq_ref[...], weight_ref[0], 1, 1)
    total = total + dot(gk_ref[...], weight_ref[1], 1, 1)
    total = total + dot(gv_ref[...], weight_ref[2], 1, 1)
    rows = keep_ref.shape[0]
    low, high = total[:rows], total[rows:]
    keep_ref[...] = low.astype(BF)
    send_ref[...] = high.astype(BF)
    gain = low * n_ref[...].astype(F32) + high * n_next_ref[...].astype(F32)
    gain_ref[...] = jnp.sum(gain, axis=0, keepdims=True)


def project_back(grad_q, grad_k, grad_v, weight, normed, half):
    count, width = grad_q.shape
    depth = weight.shape[1]
    block = pl.BlockSpec((count, width), lambda i: (half, 0))
    out = [jax.ShapeDtypeStruct((count // 2, depth), BF)] * 2
    out.append(jax.ShapeDtypeStruct((1, depth), F32))
    return pl.pallas_call(
        project_back_kernel,
        grid=(1,),
        in_specs=[
            whole_spec(grad_q),
            block,
            block,
            whole_spec(weight),
            whole_spec(normed[0]),
            whole_spec(normed[1]),
        ],
        out_specs=[whole_spec(o) for o in out],
        out_shape=out,
        compiler_params=params(1),
        cost_estimate=cost(6 * count * depth * width, 8 * 2**20),
        name="project_back",
    )(grad_q, grad_k, grad_v, weight, *normed)


def slab_gather(own):
    far = exchange(own, "col", 2)
    near = exchange(own, "col", 1)
    return [own, near, far, exchange(far, "col", 1)]


def send_far(keep, send):
    paired = keep.astype(F32) + exchange(send, "col", 1).astype(F32)
    return exchange(paired.astype(BF), "col", 2).astype(F32)


def sum_near(keep, send):
    return keep.astype(F32) + exchange(send, "col", 1).astype(F32)


def layer_norm(inputs, gain):
    average = jnp.mean(inputs, axis=-1, keepdims=True)
    centred = inputs - average
    variance = jnp.mean(centred * centred, axis=-1, keepdims=True)
    return centred * lax.rsqrt(variance + EPSILON) * gain


def rotary_tables(places):
    halfway = HEAD_DIM // 2
    inverse = ROPE_BASE ** (-(jnp.arange(halfway).astype(F32) * 2.0) / HEAD_DIM)
    angles = places.astype(F32)[:, None] * inverse[None, :]
    cosines, sines = jnp.cos(angles), jnp.sin(angles)
    return (
        jnp.concatenate([cosines] * (PAIR // halfway), axis=1),
        jnp.concatenate([-sines, sines] * (PAIR // HEAD_DIM), axis=1),
    )


def per_device(
    activations,
    upstream_grad,
    w_qkv,
    w_out_attn,
    w_in,
    w_out_mlp,
    gain_attn,
    gain_mlp,
    lengths,
    seq_order,
):
    own_rows, width = activations.shape
    shard_width = w_qkv.shape[0]
    heads_width = w_qkv.shape[2]
    units = w_out_mlp.shape[0]
    row_count = lax.axis_size("row")
    slab_index = lax.axis_index("dp") * row_count + lax.axis_index("row")
    col_index = lax.axis_index("col")
    slab_ids = jnp.arange(seq_order.shape[0])
    seq_id = jnp.sum(jnp.where(slab_ids == slab_index, seq_order, 0))
    slot_len = jnp.sum(jnp.where(slab_ids == seq_id, lengths, 0))
    places = ((col_index ^ jnp.arange(4))[:, None] * own_rows + jnp.arange(own_rows)).reshape(-1)
    key_valid = places < slot_len
    own_valid = key_valid[:own_rows, None]
    cos_table, sin_table = rotary_tables(places)
    bias = jnp.broadcast_to(jnp.where(key_valid, 0.0, NEG_LARGE)[:, None], (places.shape[0], PAIR))
    bias = bias.astype(BF)

    bits = bits_of("dp") + bits_of("row")
    far_first = bits_of("dp") + bits_of("row")
    row_first = bits_of("row") + bits_of("dp")
    table_far, table_row = source_shards(far_first), source_shards(row_first)

    qkv = jnp.transpose(w_qkv, (1, 0, 2))
    pieces_a = gather_blocks(qkv[:, :, :LANES], far_first)
    pieces_b = gather_blocks(qkv[:, :, LANES:], row_first)
    attn_pieces = gather_blocks(w_out_attn, far_first)
    in_block = jnp.transpose(w_in, (1, 2, 0)).reshape(2 * units, shard_width)
    in_pieces = gather_blocks(in_block, far_first)
    mlp_pieces = gather_blocks(w_out_mlp, far_first)

    inputs = activations.astype(F32)
    norm_one, norm_one_back = jax.vjp(layer_norm, inputs, gain_attn)
    n1 = slab_gather(norm_one.astype(BF))
    grad_out = jnp.where(own_valid, upstream_grad.astype(F32), 0.0)
    go = slab_gather(grad_out.astype(BF))
    queries, key_rows, value_rows, full_qkv = project(
        n1, pieces_a, table_far, pieces_b, table_row, cos_table, sin_table
    )
    att_far, prob_far = attend(bias, queries, key_rows, value_rows, 1)
    keep, send, full_attn = branch(att_far, attn_pieces, table_far)
    branch_far = send_far(keep, send)
    att_near, prob_near = attend(bias, queries, key_rows, value_rows, 0)
    keep, send, _ = branch(att_near, [full_attn[None]], jnp.zeros((1,), jnp.int32))
    hidden = inputs + (sum_near(keep, send) + branch_far)

    norm_two, norm_two_back = jax.vjp(layer_norm, hidden, gain_mlp)
    n2 = slab_gather(norm_two.astype(BF))
    near = feed(n2[:2], go[:2], in_pieces, mlp_pieces, table_far)
    far = feed(n2[2:], go[2:], in_pieces, mlp_pieces, table_far)
    grad_normed_two = send_far(*far[5:]) + sum_near(*near[5:])
    mlp_out = send_far(*far[:2]) + sum_near(*near[:2])
    block_out = jnp.where(own_valid, hidden + mlp_out, 0.0).astype(BF)
    hidden_part, grad_gain_two = norm_two_back(grad_normed_two)
    grad_hidden = grad_out + hidden_part
    gh = slab_gather(grad_hidden.astype(BF))

    x_order, z_order = far_first[::-1], row_first[::-1]
    keep, send = wide_grad([([near[2], far[2]], go)], x_order, bits, shard_width)
    grad_w_out_mlp = scatter_rest(keep, exchange(send, *x_order[0]), x_order, bits)
    groups = [([near[3], far[3]], n2), ([near[4], far[4]], n2)]
    keep, send = wide_grad(groups, x_order, bits, shard_width)
    grad_w_in = scatter_rest(keep, exchange(send, *x_order[0]), x_order, bits)

    common = (queries, key_rows, value_rows, cos_table, sin_table)
    gq_near, k_sum, v_sum = attend_back(prob_near, gh[:2], full_attn, att_near, *common, 0)
    gq_far, grad_k, grad_v = attend_back(
        prob_far, gh[2:], full_attn, att_far, *common, 1, (k_sum, v_sum)
    )
    keep, send, gain_far = project_back(gq_far, grad_k, grad_v, full_qkv, n1[2:], 1)
    sum_far = send_far(keep, send)
    keep, send, gain_near = project_back(gq_near, grad_k, grad_v, full_qkv, n1[:2], 0)
    grad_normed_one = sum_far + sum_near(keep, send)
    keep, send = wide_grad([([att_near, att_far], gh)], x_order, bits, shard_width)
    grad_w_out_attn = scatter_rest(keep, exchange(send, *x_order[0]), x_order, bits)
    grads = (gq_near, gq_far, grad_k, grad_v)
    keep, send = tall_grad(n1, grads, 0, x_order, bits, shard_width)
    grad_a = scatter_rest(keep, exchange(send, *x_order[0]), x_order, bits)
    keep, send = tall_grad(n1, grads, 1, z_order, bits, shard_width)
    grad_b = scatter_rest(keep, exchange(send, *z_order[0]), z_order, bits)
    input_part, _ = norm_one_back(grad_normed_one)
    grad_input = (grad_hidden + input_part).astype(BF)

    gains = jnp.stack([(gain_far + gain_near)[0] / gain_attn, grad_gain_two])
    for axis, bit in bits_of("col") + bits:
        gains = gains + exchange(gains, axis, bit)
    return (
        block_out,
        grad_input,
        jnp.transpose(jnp.concatenate([grad_a, grad_b], 2), (1, 0, 2)),
        grad_w_out_attn,
        jnp.transpose(grad_w_in.reshape(2, units, shard_width), (2, 0, 1)),
        grad_w_out_mlp,
        gains[0],
        gains[1],
    )


def solution(mesh):
    rows = P(("dp", "row", "col"), None)
    tall = P(("dp", "row"), None, "col")
    wide = P("col", ("dp", "row"))
    return jax.shard_map(
        per_device,
        mesh=mesh,
        in_specs=(rows, rows, tall, wide, tall, wide, P(), P(), P(), P()),
        out_specs=(rows, rows, tall, wide, tall, wide, P(), P()),
        check_vma=False,
    )
```
